32 devices in a mesh: runs: 2 (over y), tile: 4 (over z), layer: 2 (over x), star: 2 (over core).
Axes of the slice: x: 2, y: 2, z: 4, core: 2. Of those that a mesh axis runs over, the one named last changes fastest.
Arguments:
- screens: float32 [12, 384, 1536], P(('runs', 'layer'), 'tile'), parts along dimension 0, may hold values from -6 to 6
- layer_weight: float32 [12], P(('runs', 'layer')), parts along dimension 0, may hold values from 0.3 to 1
- wind_row: int32 [12], P('runs'), parts along dimension 0, may hold values from -4 to 4, as said below
- wind_col: int32 [12], P('runs'), parts along dimension 0, may hold values from -4 to 4, as said below
- foot_row: int32 [6, 6], replicated, may hold values from -80 to 79, as said below
- foot_col: int32 [6, 6], replicated, may hold values from -80 to 79, as said below
- frac_row: float32 [6, 6], replicated, may hold values from 0 to 1
- frac_col: float32 [6, 6], replicated, may hold values from 0 to 1
- amplitude: float32 [384, 1536], P('tile', 'layer'), may hold values from 0.5 to 2
- valid: int32 [24, 96], P('tile', 'layer'), may hold values 0 or 1
- recon_matrix: bfloat16 [6, 2, 24, 96, 2688], P('star', None, 'tile', 'layer'), may hold values from -0.0390625 to 0.0390625
- prev_recon: float32 [5376], P('runs'), parts along dimension 0, may hold values from -6 to 6
Outputs:
- shifted: float32 [12, 384, 1536], P(('runs', 'layer'), 'tile'), parts along dimension 0
- slopes: float32 [12, 2, 24, 96], P(('runs', 'star'), None, 'tile', 'layer'), parts along dimension 0
- commands: float32 [5376], P('runs'), parts along dimension 0
The draws below stay inside these ranges and needn't reach their ends.
There are 2 independent parts, one for each index of `runs`. The reference program is written for one: setup_inputs(seed, part) draws one part's arguments, and reference() takes and returns one part's arrays. A program takes and returns all parts, laid end to end along the dimension named above; an argument that names none is the same for every part. Nothing has to cross between parts.
Inputs may be any that keep to these rules, and one draw needn't show every extreme that they name: `wind_row`: some layer takes 4 and another takes -4. `wind_col`: some layer takes 4 and another takes -4. `foot_row`: some star and layer take -80 and another takes 80 - 1. `foot_col`: some star and layer take -80 and another takes 80 - 1.
All inputs are finite; a program needn't handle non-finite values. No bound on the sum of `valid` on one device may be relied on, other than what follows from the above.
Results may differ from the reference program's by a relative error of at most 0.0019.
Values sent between devices are 32-bit elements; how exact they have to be, the bound alone decides.
A program may use at most 64 MiB of HBM per device.

```python
import math
import jax
import jax.numpy as jnp

PIX = 16
PAD = 32
SUB_COLS = 96
NACT = 2688
WIND = 4
FOOT = 80
LAYERS = 6
STARS = 6
SUBROWS = 24
ROWS = 384
COLS = 1536


def with_ends(key, count, lowest_value, highest_value):
    first_key, second_key, third_key = jax.random.split(key, 3)
    values = jax.random.randint(first_key, (count,), lowest_value, highest_value + 1)
    top_place = jax.random.randint(second_key, (), 0, count)
    stride = jax.random.randint(third_key, (), 1, count)
    low_place = jnp.mod(top_place + stride, count)
    places = jnp.arange(count)
    values = jnp.where(places == top_place, highest_value, values)
    values = jnp.where(places == low_place, lowest_value, values)
    return values.astype(jnp.int32)


def draw_wind_row(key, part):
    return with_ends(jax.random.fold_in(key, 7), LAYERS, -WIND, WIND)


def draw_wind_col(key, part):
    return with_ends(jax.random.fold_in(key, 11), LAYERS, -WIND, WIND)


def draw_foot_row(key, part):
    return with_ends(jax.random.fold_in(key, 13), STARS * LAYERS, -FOOT, FOOT - 1).reshape(STARS, LAYERS)


def draw_foot_col(key, part):
    return with_ends(jax.random.fold_in(key, 17), STARS * LAYERS, -FOOT, FOOT - 1).reshape(STARS, LAYERS)


def touch_ends(result, rng, low, high):
    longest = result.shape.index(max(result.shape))
    spots = []
    for shift in (0, 1):
        where = [jax.random.randint(jax.random.fold_in(rng, axis), (), 0, length) for axis, length in enumerate(result.shape)]
        where[longest] = (where[longest] + shift) % result.shape[longest]
        spots.append(tuple(where))
    return result.at[spots[0]].set(low).at[spots[1]].set(high)


def shard_levels(stream_key, extent, pieces, low, high):
    gain, own = 1.0, jax.random.fold_in(stream_key, 6)
    for position, blocks in pieces:
        heights = jnp.exp(jax.random.uniform(jax.random.fold_in(own, position), (blocks,), jnp.float32, low / len(pieces), high / len(pieces)))
        gain = gain * jnp.repeat(heights, extent[position] // blocks).reshape([-1 if axis == position else 1 for axis in range(len(extent))])
    return gain


def scatter_about(own_key, extent, scale, most, cuts=(), dtype=jnp.bfloat16):
    values = scale * jax.random.normal(own_key, extent, jnp.float32)
    if cuts:
        values = values * shard_levels(own_key, extent, cuts, -0.22, 0.18)
    return jnp.clip(values, -most, most).astype(dtype)


def setup_inputs(seed: int = 0, part: int = 0) -> dict:
    key_list = jax.random.split(jax.random.key(seed), 13)
    part_splits = jax.random.split(jax.random.fold_in(key_list[12], part), 13)
    screens = scatter_about(part_splits[0], (LAYERS, ROWS, COLS), 1.0, 6.0, ((0, 2), (1, 4)), jnp.float32)
    layer_weight = jnp.clip(jnp.exp(math.log(1.0) - 1.2039728 * jax.random.uniform(part_splits[1], (LAYERS,), jnp.float32) ** shard_levels(part_splits[1], (LAYERS,), ((0, 2),), -0.2, 0.2)), 0.3, 1.0)
    wind_row = draw_wind_row(jax.random.fold_in(jax.random.fold_in(key_list[12], part), 71), part)
    wind_col = draw_wind_col(jax.random.fold_in(jax.random.fold_in(key_list[12], part), 71), part)
    foot_row = draw_foot_row(jax.random.fold_in(key_list[12], 71), part)
    foot_col = draw_foot_col(jax.random.fold_in(key_list[12], 71), part)
    frac_row = jnp.clip(jax.random.uniform(key_list[6], (STARS, LAYERS), jnp.float32, 0.0, 1.0), 0.0, 1.0)
    frac_col = jnp.clip(jax.random.uniform(key_list[7], (STARS, LAYERS), jnp.float32, 0.0, 1.0), 0.0, 1.0)
    amplitude = jnp.clip(jnp.exp(math.log(2.0) - 1.3862944 * jax.random.uniform(key_list[8], (ROWS, COLS), jnp.float32) ** shard_levels(key_list[8], (ROWS, COLS), ((0, 4), (1, 2)), -0.2, 0.2)), 0.5, 2.0)
    valid = touch_ends((jax.random.randint(key_list[9], (SUBROWS, SUB_COLS), 0, 4) < 3).astype(jnp.int32), jax.random.fold_in(key_list[9], 1), 0, 1)
    recon_matrix = scatter_about(key_list[10], (STARS, 2, SUBROWS, SUB_COLS, NACT), (STARS * 2 * SUBROWS * SUB_COLS) ** -0.5, 0.0390625, ((0, 2), (2, 4), (3, 2)))
    prev_recon = scatter_about(part_splits[11], (NACT,), 1.0, 6.0, (), jnp.float32)
    return {"screens": screens, "layer_weight": layer_weight, "wind_row": wind_row, "wind_col": wind_col, "foot_row": foot_row, "foot_col": foot_col, "frac_row": frac_row, "frac_col": frac_col, "amplitude": amplitude, "valid": valid, "recon_matrix": recon_matrix, "prev_recon": prev_recon}


def star_images(phase, amplitude, valid):
    field = amplitude * jnp.cos(phase) + 1j * (amplitude * jnp.sin(phase))
    blocks = field.reshape(SUBROWS, PIX, SUB_COLS, PIX).transpose(0, 2, 1, 3)
    spectrum = jnp.fft.fft2(blocks, s=(PAD, PAD))
    intensity = jnp.real(spectrum) ** 2 + jnp.imag(spectrum) ** 2
    centred = (jnp.mod(jnp.arange(PAD) + PAD // 2, PAD) - PAD // 2).astype(jnp.float32)
    summed = jnp.sum(intensity, axis=(2, 3))
    along_rows = jnp.sum(intensity * centred[:, None], axis=(2, 3)) / summed
    along_cols = jnp.sum(intensity * centred[None, :], axis=(2, 3)) / summed
    return jnp.stack([along_rows, along_cols]) * valid.astype(jnp.float32)


def reference(screens, layer_weight, wind_row, wind_col, foot_row, foot_col, frac_row, frac_col, amplitude, valid, recon_matrix, prev_recon):
    shifted = jnp.stack([jnp.roll(screens[l], (wind_row[l], wind_col[l]), axis=(0, 1)) for l in range(LAYERS)])
    results = []
    for g in range(STARS):
        pupil = jnp.zeros((ROWS, COLS), jnp.float32)
        for l in range(LAYERS):
            row_frac = frac_row[g, l]
            col_frac = frac_col[g, l]
            anchor = jnp.roll(shifted[l], (-foot_row[g, l], -foot_col[g, l]), axis=(0, 1))
            lower = jnp.roll(anchor, -1, axis=0)
            beside = jnp.roll(anchor, -1, axis=1)
            corner = jnp.roll(lower, -1, axis=1)
            sampled = ((1.0 - row_frac) * (1.0 - col_frac) * anchor + row_frac * (1.0 - col_frac) * lower
                       + (1.0 - row_frac) * col_frac * beside + row_frac * col_frac * corner)
            pupil = pupil + layer_weight[l] * sampled
        results.append(star_images(pupil, amplitude, valid))
    slopes = jnp.stack(results)
    recon = jnp.dot(slopes.astype(jnp.bfloat16).reshape(1, -1), recon_matrix.reshape(-1, NACT), preferred_element_type=jnp.float32)[0]
    commands = 2.0 * recon - prev_recon
    return shifted, slopes, commands
```

```python
import functools
import math

import jax
import jax.numpy as jnp
from jax import lax
from jax.experimental import pallas as pl
from jax.experimental.pallas import tpu as pltpu
from jax.sharding import PartitionSpec as P

PIX = 16
PAD = 32
WIND = 4
FOOT = 80
LANES = 128
HALO = -(-(WIND + FOOT + 1) // 8) * 8
MESH = pl.DeviceIdType.MESH
ANY = pl.BlockSpec(memory_space=pl.ANY)
SMEM = pl.BlockSpec(memory_space=pltpu.SMEM)
VMEM = pl.BlockSpec(memory_space=pltpu.VMEM)


def greet(peers):
    barrier = pltpu.get_barrier_semaphore()
    for peer in peers:
        pl.semaphore_signal(barrier, inc=1, device_id=peer, device_id_type=MESH)
    pl.semaphore_wait(barrier, len(peers))


def halo_kernel(tiles, cores, screens, above, below, zsend, zrecv, csend, crecv):
    tile, core = lax.axis_index("tile"), lax.axis_index("star")
    up, down = lax.rem(tile + 1, tiles), lax.rem(tile + tiles - 1, tiles)
    lays, rows, cols = screens.shape
    part = cols // cores
    mine = pl.ds(pl.multiple_of(core * part, LANES), part)
    partners = [lax.rem(core + k, cores) for k in range(1, cores)]
    greet([{"tile": up}, {"tile": down}] + [{"star": p} for p in partners])
    first = []
    for j in range(lays):
        for d, (start, target, peer) in enumerate(((rows - HALO, above, up), (0, below, down))):
            i = 2 * j + d
            copy = pltpu.make_async_remote_copy(
                src_ref=screens.at[j, pl.ds(start, HALO), mine],
                dst_ref=target.at[j, :, mine],
                send_sem=zsend.at[i],
                recv_sem=zrecv.at[i],
                device_id={"tile": peer},
                device_id_type=MESH,
            )
            copy.start()
            first.append((i, j, target, copy))
    second = []
    for i, j, target, copy in first:
        copy.wait_recv()
        for k, p in enumerate(partners):
            n = i * (cores - 1) + k
            block = target.at[j, :, mine]
            forward = pltpu.make_async_remote_copy(
                src_ref=block,
                dst_ref=block,
                send_sem=csend.at[n],
                recv_sem=crecv.at[n],
                device_id={"star": p},
                device_id_type=MESH,
            )
            forward.start()
            second.append(forward)
    for i, j, target, copy in first:
        copy.wait_send()
    for forward in second:
        forward.wait()


def halos(screens):
    tiles, cores = lax.axis_size("tile"), lax.axis_size("star")
    lays, rows, cols = screens.shape
    side = jax.ShapeDtypeStruct((lays, HALO, cols), screens.dtype)
    count = 2 * lays
    return pl.pallas_call(
        functools.partial(halo_kernel, tiles, cores),
        out_shape=(side, side),
        in_specs=[ANY],
        out_specs=(ANY, ANY),
        scratch_shapes=[
            pltpu.SemaphoreType.DMA((count,)),
            pltpu.SemaphoreType.DMA((count,)),
            pltpu.SemaphoreType.DMA((count * max(1, cores - 1),)),
            pltpu.SemaphoreType.DMA((count * max(1, cores - 1),)),
        ],
        compiler_params=pltpu.CompilerParams(collective_id=0, has_side_effects=True),
        name="halo",
    )(screens)


def pupil_kernel(
    blocks, stars, ints, floats, screens, above, below, partial, shifted, field, sems
):
    lays, rows, cols = screens.shape
    strips = cols // LANES
    copies = []
    for n, (source, at) in enumerate(((above, 0), (screens, HALO), (below, HALO + rows))):
        size = source.shape[1]
        for m in range(strips + 2):
            copies.append(
                pltpu.make_async_copy(
                    source.at[:, :, pl.ds((m - 1) % strips * LANES, LANES)],
                    field.at[:, m, pl.ds(at, size), :],
                    sems.at[(strips + 2) * n + m],
                )
            )
    for copy in copies:
        copy.start()
    for copy in copies:
        copy.wait()
    per_block = strips // blocks
    groups = rows // 8
    lane = lax.broadcasted_iota(jnp.int32, (8, LANES), 1)

    def window(j, row, base):
        return [field[j, base + k, pl.ds(row, 8), :] for k in range(strips + 1)]

    def moved(j, i):
        row = HALO + i * 8 - ints[0, j]
        start = LANES - ints[1, j]
        base = start // LANES
        turn = start - base * LANES
        values = window(j, row, base)
        rolled = [
            pltpu.roll(v, (LANES - turn) & (LANES - 1), 1) for v in values
        ]
        keep = lane < LANES - turn
        for k in range(strips):
            shifted[j, pl.ds(i * 8, 8), pl.ds(k * LANES, LANES)] = jnp.where(
                keep, rolled[k], rolled[k + 1]
            )

    def move_step(n, carry):
        j = n // groups
        moved(j, n - j * groups)
        return carry

    lax.fori_loop(0, lays * groups, move_step, 0)

    def pupil_step(n, carry):
        g = n // groups
        i = n - g * groups
        total = [None] * strips
        for j in range(lays):
            row = HALO + i * 8 + ints[2 + 2 * g, j] - ints[0, j]
            start = LANES + ints[3 + 2 * g, j] - ints[1, j]
            base = start // LANES
            turn = start - base * LANES
            weight = floats[0, j]
            a, b = floats[1 + 2 * g, j], floats[2 + 2 * g, j]
            top, bottom = weight * (1.0 - a), weight * a
            values = [
                top * x + bottom * y
                for x, y in zip(window(j, row, base), window(j, row + 1, base))
            ]
            near = [pltpu.roll(v, (LANES - turn) & (LANES - 1), 1) for v in values]
            far = [pltpu.roll(v, LANES - 1 - turn, 1) for v in values]
            keep_near = lane < LANES - turn
            keep_far = lane < LANES - 1 - turn
            for k in range(strips):
                term = (1.0 - b) * jnp.where(keep_near, near[k], near[k + 1]) + b * jnp.where(
                    keep_far, far[k], far[k + 1]
                )
                total[k] = term if total[k] is None else total[k] + term
        for k in range(strips):
            q, w = divmod(k, per_block)
            partial[q, g, pl.ds(i * 8, 8), pl.ds(w * LANES, LANES)] = total[k]
        return carry

    lax.fori_loop(0, stars * groups, pupil_step, 0)


def pupils(ints, floats, screens, above, below, stars):
    blocks = lax.axis_size("layer")
    lays, rows, cols = screens.shape
    return pl.pallas_call(
        functools.partial(pupil_kernel, blocks, stars),
        out_shape=(
            jax.ShapeDtypeStruct((blocks, stars, rows, cols // blocks), jnp.float32),
            jax.ShapeDtypeStruct((lays, rows, cols), jnp.float32),
        ),
        in_specs=[SMEM, SMEM, ANY, ANY, ANY],
        out_specs=(VMEM, VMEM),
        scratch_shapes=[
            pltpu.VMEM((lays, cols // LANES + 2, rows + 2 * HALO, LANES), jnp.float32),
            pltpu.SemaphoreType.DMA((3 * (cols // LANES + 2),)),
        ],
        name="pupil",
    )(ints, floats, screens, above, below)


def swap_kernel(blocks, partial, received, send, recv):
    me = lax.axis_index("layer")
    peers = [lax.rem(me + k, blocks) for k in range(1, blocks)]
    greet([{"layer": p} for p in peers])
    copies = []
    for k, p in enumerate(peers):
        copy = pltpu.make_async_remote_copy(
            src_ref=partial.at[p],
            dst_ref=received.at[k],
            send_sem=send.at[k],
            recv_sem=recv.at[k],
            device_id={"layer": p},
            device_id_type=MESH,
        )
        copy.start()
        copies.append(copy)
    for copy in copies:
        copy.wait()


def swap(partial):
    blocks = partial.shape[0]
    return pl.pallas_call(
        functools.partial(swap_kernel, blocks),
        out_shape=jax.ShapeDtypeStruct((blocks - 1,) + partial.shape[1:], jnp.float32),
        in_specs=[ANY],
        out_specs=ANY,
        scratch_shapes=[
            pltpu.SemaphoreType.DMA((blocks - 1,)),
            pltpu.SemaphoreType.DMA((blocks - 1,)),
        ],
        compiler_params=pltpu.CompilerParams(collective_id=1, has_side_effects=True),
        name="swap",
    )(partial)


def sine_cosine(x):
    turns = jnp.floor(x * (2.0 / math.pi) + 0.5)
    r = x - turns * 1.5703125
    r = r - turns * 4.837512969970703125e-4
    r = r - turns * 7.54978995489188216e-8
    z = r * r
    s = r + r * z * (-1.6666654611e-1 + z * (8.3321608736e-3 - z * 1.9515295891e-4))
    c = 1.0 - 0.5 * z + z * z * (
        4.166664568298827e-2 + z * (-1.388731625493765e-3 + z * 2.443315711809948e-5)
    )
    quadrant = turns.astype(jnp.int32)
    odd = (quadrant & 1) == 1
    sine = jnp.where(odd, c, s)
    cosine = jnp.where(odd, s, c)
    sine = jnp.where((quadrant & 2) == 2, -sine, sine)
    cosine = jnp.where(((quadrant + 1) & 2) == 2, -cosine, cosine)
    return sine, cosine


def exact_dot(x, y):
    return jnp.dot(x, y, precision=lax.Precision.HIGHEST, preferred_element_type=jnp.float32)


def slope_kernel(
    blocks, partial, received, amplitude, valid, row_table, row_alt, col_table, gather,
    slopes, own, real, imag, sem,
):
    me = lax.axis_index("layer")
    copy = pltpu.make_async_copy(partial.at[me], own, sem)
    copy.start()
    stars, rows, cols = own.shape
    subs = rows // PIX

    def per_sub(values):
        return jnp.sum(values.reshape(subs, PIX, cols), axis=1)

    power = amplitude[...]
    scale = exact_dot(per_sub(power * power), gather[...])
    scale = valid[...].astype(jnp.float32) / (scale * PAD)
    copy.wait()
    for g in range(stars):

        def step(i, carry):
            at = pl.ds(pl.multiple_of(i * PIX, PIX), PIX)
            phase = own[g, at, :]
            for k in range(blocks - 1):
                phase = phase + received[k, g, at, :]
            sine, cosine = sine_cosine(phase)
            amp = amplitude[at, :]
            real[at, :] = amp * cosine
            imag[at, :] = amp * sine
            return carry

        lax.fori_loop(0, subs, step, 0)
        a, b = real[...], imag[...]
        along = per_sub(a * exact_dot(row_table[...], b))
        alt_a, alt_b = exact_dot(row_alt[...], a)[:subs], exact_dot(row_alt[...], b)[:subs]
        down = 2.0 * along - PIX * (alt_a * alt_a + alt_b * alt_b)
        slopes[g, 0] = exact_dot(down, gather[...]) * scale
        pieces = []
        for k in range(cols // LANES):
            at = slice(k * LANES, (k + 1) * LANES)
            left, right = a[:, at], b[:, at]
            turned = exact_dot(right, col_table[...])
            other = exact_dot(left, col_table[:, LANES:])
            alt = turned[:, LANES:]
            pieces.append(2.0 * left * turned[:, :LANES] - (alt * alt + other * other))
        across = per_sub(jnp.concatenate(pieces, axis=1))
        slopes[g, 1] = exact_dot(across, gather[...]) * scale


def tables(rows, cols):
    def block_diagonal(count, block):
        return jnp.kron(jnp.eye(count, dtype=jnp.float32), block)

    index = jnp.arange(PIX, dtype=jnp.int32)
    gap = index[:, None] - index[None, :]
    angle = jnp.where(gap == 0, 1, gap).astype(jnp.float32) * (math.pi / PAD)
    sign = jnp.where(gap % 2 == 0, 1.0, -1.0)
    table = jnp.where(gap == 0, 0.0, PIX * sign * jnp.cos(angle) / jnp.sin(angle))
    alternate = jnp.where(index % 2 == 0, 1.0, -1.0).astype(jnp.float32)
    subs = rows // PIX
    row_table = block_diagonal(subs, table)
    row_alt = block_diagonal(subs, alternate[None, :])
    row_alt = jnp.pad(row_alt, ((0, -subs % 8), (0, 0)))
    per = LANES // PIX
    spread = jnp.zeros((PIX, PIX), jnp.float32).at[:, 0].set(4.0 * alternate)
    col_table = jnp.concatenate(
        [block_diagonal(per, table.T), block_diagonal(per, spread)], axis=1
    )
    gather = block_diagonal(cols // PIX, jnp.ones((PIX, 1), jnp.float32))
    return row_table, row_alt, col_table, gather


def slopes_of(partial, received, amplitude, valid):
    blocks, stars, rows, cols = partial.shape
    subs = valid.shape
    return pl.pallas_call(
        functools.partial(slope_kernel, blocks),
        out_shape=jax.ShapeDtypeStruct((stars, 2) + subs, jnp.float32),
        in_specs=[ANY] + [VMEM] * 7,
        out_specs=VMEM,
        scratch_shapes=[
            pltpu.VMEM((stars, rows, cols), jnp.float32),
            pltpu.VMEM((rows, cols), jnp.float32),
            pltpu.VMEM((rows, cols), jnp.float32),
            pltpu.SemaphoreType.DMA,
        ],
        name="slopes",
    )(partial, received, amplitude, valid, *tables(rows, cols))


def reduce_kernel(tiles, blocks, cores, terms, out, near, far, nsend, nrecv, fsend, frecv):
    tile, layer, core = (lax.axis_index(n) for n in ("tile", "layer", "star"))
    count = blocks * cores
    me = layer * cores + core
    near_peers = []
    for k in range(1, count):
        rank = lax.rem(me + k, count)
        near_peers.append({"layer": rank // cores, "star": lax.rem(rank, cores)})
    far_peers = [{"tile": lax.rem(tile + k, tiles)} for k in range(1, tiles)]
    greet(near_peers + far_peers)
    copies = []
    for k, peer in enumerate(near_peers):
        copy = pltpu.make_async_remote_copy(
            src_ref=terms,
            dst_ref=near.at[me],
            send_sem=nsend.at[k],
            recv_sem=nrecv.at[k],
            device_id=peer,
            device_id_type=MESH,
        )
        copy.start()
        copies.append(copy)
    near[me] = terms[...]
    for copy in copies:
        copy.wait()
    total = near[0]
    for k in range(1, count):
        total = total + near[k]
    far[tile] = total
    copies = []
    for k, peer in enumerate(far_peers):
        copy = pltpu.make_async_remote_copy(
            src_ref=far.at[tile],
            dst_ref=far.at[tile],
            send_sem=fsend.at[k],
            recv_sem=frecv.at[k],
            device_id=peer,
            device_id_type=MESH,
        )
        copy.start()
        copies.append(copy)
    for copy in copies:
        copy.wait()
    total = far[0]
    for k in range(1, tiles):
        total = total + far[k]
    out[...] = total


def reduce_all(terms):
    tiles, blocks, cores = (lax.axis_size(n) for n in ("tile", "layer", "star"))
    count = blocks * cores
    return pl.pallas_call(
        functools.partial(reduce_kernel, tiles, blocks, cores),
        out_shape=jax.ShapeDtypeStruct(terms.shape, jnp.float32),
        in_specs=[VMEM],
        out_specs=VMEM,
        scratch_shapes=[
            pltpu.VMEM((count,) + terms.shape, jnp.float32),
            pltpu.VMEM((tiles,) + terms.shape, jnp.float32),
            pltpu.SemaphoreType.DMA((count - 1,)),
            pltpu.SemaphoreType.DMA((count - 1,)),
            pltpu.SemaphoreType.DMA((tiles - 1,)),
            pltpu.SemaphoreType.DMA((tiles - 1,)),
        ],
        compiler_params=pltpu.CompilerParams(collective_id=2, has_side_effects=True),
        name="reduce",
    )(terms)


def body(
    screens,
    layer_weight,
    wind_row,
    wind_col,
    foot_row,
    foot_col,
    frac_row,
    frac_col,
    amplitude,
    valid,
    recon_matrix,
    prev_recon,
):
    lays = screens.shape[0]
    stars = recon_matrix.shape[0]
    layer_start = lax.axis_index("layer") * lays
    star_start = lax.axis_index("star") * stars

    def own(table):
        return lax.dynamic_slice(table, (star_start, layer_start), (stars, lays))

    def pairs(first, second):
        return jnp.stack([own(first), own(second)], axis=1).reshape(2 * stars, lays)

    winds = [lax.dynamic_slice_in_dim(w, layer_start, lays, 0)[None] for w in (wind_row, wind_col)]
    ints = jnp.concatenate(winds + [pairs(foot_row, foot_col)], axis=0)
    floats = jnp.concatenate([layer_weight[None], pairs(frac_row, frac_col)], axis=0)
    above, below = halos(screens)
    partial, shifted = pupils(ints, floats, screens, above, below, stars)
    received = swap(partial)
    slopes = slopes_of(partial, received, amplitude, valid)
    local_terms = jnp.dot(
        slopes.astype(jnp.bfloat16).reshape(1, -1),
        recon_matrix.reshape(-1, recon_matrix.shape[-1]),
        preferred_element_type=jnp.float32,
    )
    recon = reduce_all(local_terms)[0]
    commands = 2.0 * recon - prev_recon
    return (shifted, slopes, commands)


def solution(mesh):
    return jax.shard_map(
        body,
        mesh=mesh,
        in_specs=(
            P(("runs", "layer"), "tile", None),
            P(("runs", "layer")),
            P("runs"),
            P("runs"),
            P(),
            P(),
            P(),
            P(),
            P("tile", "layer"),
            P("tile", "layer"),
            P("star", None, "tile", "layer", None),
            P("runs"),
        ),
        out_specs=(
            P(("runs", "layer"), "tile", None),
            P(("runs", "star"), None, "tile", "layer"),
            P("runs"),
        ),
        check_vma=False,
    )
```

```python
import functools
import math

import jax
import jax.numpy as jnp
import numpy as np
from jax import lax
from jax.experimental import pallas as pl
from jax.experimental.pallas import tpu as pltpu
from jax.sharding import PartitionSpec as P

PIX = 16
PAD = 32
WIND = 4
FOOT = 80
LANES = 128
HALO = -(-(WIND + FOOT + 1) // 8) * 8
MESH = pl.DeviceIdType.MESH
ANY = pl.BlockSpec(memory_space=pl.ANY)
SMEM = pl.BlockSpec(memory_space=pltpu.SMEM)
VMEM = pl.BlockSpec(memory_space=pltpu.VMEM)


def greet(peers):
    barrier = pltpu.get_barrier_semaphore()
    for peer in peers:
        pl.semaphore_signal(barrier, inc=1, device_id=peer, device_id_type=MESH)
    pl.semaphore_wait(barrier, len(peers))


def flow_kernel(
    tiles, cores, blocks, stars, ints, floats, screens, share, shifted,
    field, land, outbox, inbox, zsend, zrecv, csend, crecv, xsend, xrecv, local,
):
    tile, core, layer = (lax.axis_index(n) for n in ("tile", "star", "layer"))
    up, down = lax.rem(tile + 1, tiles), lax.rem(tile + tiles - 1, tiles)
    partners = [lax.rem(core + k, cores) for k in range(1, cores)]
    peers = [lax.rem(layer + k, blocks) for k in range(1, blocks)]
    lays, rows, cols = screens.shape
    strips = cols // LANES
    per_block = strips // blocks
    unit = share.shape[2] // LANES // inbox.shape[1]
    units = inbox.shape[1]
    groups = rows // 8
    first = (layer + 1) * per_block + strips - 1

    def column(n):
        return pl.ds(pl.multiple_of(lax.rem(first + n, strips) * LANES, LANES), LANES)

    copies = []
    for n in range(strips + 2):
        copy = pltpu.make_async_copy(
            screens.at[:, :, column(n % strips)],
            field.at[:, n, pl.ds(HALO, rows), :],
            local.at[n],
        )
        copy.start()
        copies.append(copy)
    greet(
        [{"tile": up}, {"tile": down}]
        + [{"star": p} for p in partners]
        + [{"layer": p} for p in peers]
    )
    sends = []
    for m in range(strips // cores):
        n = m * cores + core
        pair = []
        for d, (start, peer) in enumerate(((rows - HALO, up), (0, down))):
            copy = pltpu.make_async_remote_copy(
                src_ref=screens.at[:, pl.ds(start, HALO), column(n)],
                dst_ref=land.at[d, n],
                send_sem=zsend.at[m, d],
                recv_sem=zrecv.at[m, d],
                device_id={"tile": peer},
                device_id_type=MESH,
            )
            copy.start()
            pair.append(copy)
        sends.append(pair)
    for copy in copies:
        copy.wait()
    lane = lax.broadcasted_iota(jnp.int32, (8, LANES), 1)

    def window(j, row, base, n):
        return [field[j, base + n + k, pl.ds(row, 8), :] for k in range(unit + 1)]

    def place(start):
        base = start // LANES
        turn = start - base * LANES
        return base, turn

    def compute(u, store):
        low = u * unit

        def move_step(i, carry):
            for j in range(lays):
                base, turn = place(LANES - ints[1, j])
                values = window(j, HALO + i * 8 - ints[0, j], base, low)
                rolled = [pltpu.roll(v, (LANES - turn) & (LANES - 1), 1) for v in values]
                keep = lane < LANES - turn
                for k in range(unit):
                    shifted[j, pl.ds(pl.multiple_of(i * 8, 8), 8), column(low + k + 1)] = jnp.where(
                        keep, rolled[k], rolled[k + 1]
                    )
            return carry

        def pupil_step(n, carry):
            g = n // groups
            i = n - g * groups
            total = [None] * unit
            for j in range(lays):
                row = HALO + i * 8 + ints[2 + 2 * g, j] - ints[0, j]
                base, turn = place(LANES + ints[3 + 2 * g, j] - ints[1, j])
                weight = floats[0, j]
                a, b = floats[1 + 2 * g, j], floats[2 + 2 * g, j]
                top, bottom = weight * (1.0 - a), weight * a
                values = [
                    top * x + bottom * y
                    for x, y in zip(window(j, row, base, low), window(j, row + 1, base, low))
                ]
                near = [pltpu.roll(v, (LANES - turn) & (LANES - 1), 1) for v in values]
                far = [pltpu.roll(v, LANES - 1 - turn, 1) for v in values]
                keep_near = lane < LANES - turn
                keep_far = lane < LANES - 1 - turn
                for k in range(unit):
                    term = (1.0 - b) * jnp.where(keep_near, near[k], near[k + 1]) + b * jnp.where(
                        keep_far, far[k], far[k + 1]
                    )
                    total[k] = term if total[k] is None else total[k] + term
            for k in range(unit):
                store(g, pl.ds(pl.multiple_of(i * 8, 8), 8), k, total[k])
            return carry

        lax.fori_loop(0, stars * groups, pupil_step, 0)
        lax.fori_loop(0, groups, move_step, 0)

    def to_outbox(u):
        def store(g, at, k, value):
            outbox[u, g, at, k * LANES : (k + 1) * LANES] = value

        return store

    def to_share(u):
        def store(g, at, k, value):
            c = u * unit + k
            share[g, at, c * LANES : (c + 1) * LANES] = value

        return store

    forwards, swaps = [], []
    done = 0
    for m in range(strips // cores):
        n = m * cores + core
        current = []
        for d in range(2):
            sends[m][d].wait_recv()
            for k, p in enumerate(partners):
                forward = pltpu.make_async_remote_copy(
                    src_ref=land.at[d, n],
                    dst_ref=land.at[d, n],
                    send_sem=csend.at[m, d, k],
                    recv_sem=crecv.at[m, d, k],
                    device_id={"star": p},
                    device_id_type=MESH,
                )
                forward.start()
                current.append(forward)
        for forward in current:
            forward.wait_recv()
        forwards.extend(current)
        have = (m + 1) * cores
        for n in range(m * cores, have):
            for to in (n, n + strips):
                if to < strips + 2:
                    for j in range(lays):
                        field[j, to, 0:HALO, :] = land[0, n, j]
                        field[j, to, HALO + rows :, :] = land[1, n, j]
        while done < units * blocks and (
            have == strips or done * unit + unit + 2 <= have
        ):
            k, w = divmod(done, units)
            if k < blocks - 1:
                compute(done, to_outbox(done))
                copy = pltpu.make_async_remote_copy(
                    src_ref=outbox.at[done],
                    dst_ref=inbox.at[k, w],
                    send_sem=xsend.at[done],
                    recv_sem=xrecv.at[done],
                    device_id={"layer": peers[k]},
                    device_id_type=MESH,
                )
                copy.start()
                swaps.append(copy)
            else:
                compute(done, to_share(w))
            done += 1
    for n, copy in enumerate(swaps):
        k, w = divmod(n, units)
        copy.wait_recv()
        at = slice(w * unit * LANES, (w + 1) * unit * LANES)
        for g in range(stars):
            share[g, :, at] = share[g, :, at] + inbox[k, w, g]
    for pair in sends:
        for copy in pair:
            copy.wait_send()
    for copy in forwards + swaps:
        copy.wait_send()


def flow(ints, floats, screens, stars):
    tiles, blocks, cores = (lax.axis_size(n) for n in ("tile", "layer", "star"))
    lays, rows, cols = screens.shape
    strips = cols // LANES
    per_block = strips // blocks
    unit = 2 if per_block % 2 == 0 else 1
    units = per_block // unit
    width = cols // blocks
    steps = strips // cores
    dma = pltpu.SemaphoreType.DMA
    return pl.pallas_call(
        functools.partial(flow_kernel, tiles, cores, blocks, stars),
        out_shape=(
            jax.ShapeDtypeStruct((stars, rows, width), jnp.float32),
            jax.ShapeDtypeStruct((lays, rows, cols), jnp.float32),
        ),
        in_specs=[SMEM, SMEM, ANY],
        out_specs=(VMEM, VMEM),
        scratch_shapes=[
            pltpu.VMEM((lays, strips + 2, rows + 2 * HALO, LANES), jnp.float32),
            pltpu.VMEM((2, strips, lays, HALO, LANES), jnp.float32),
            pltpu.VMEM((units * (blocks - 1), stars, rows, unit * LANES), jnp.float32),
            pltpu.VMEM((blocks - 1, units, stars, rows, unit * LANES), jnp.float32),
            dma((steps, 2)),
            dma((steps, 2)),
            dma((steps, 2, cores - 1)),
            dma((steps, 2, cores - 1)),
            dma((units * (blocks - 1),)),
            dma((units * (blocks - 1),)),
            dma((strips + 2,)),
        ],
        compiler_params=pltpu.CompilerParams(collective_id=0, has_side_effects=True),
        name="flow",
    )(ints, floats, screens)


def sine_cosine(x):
    turns = jnp.floor(x * (2.0 / math.pi) + 0.5)
    r = x - turns * 1.5703125
    r = r - turns * 4.837512969970703125e-4
    r = r - turns * 7.54978995489188216e-8
    z = r * r
    s = r + r * z * (-1.6666654611e-1 + z * (8.3321608736e-3 - z * 1.9515295891e-4))
    c = 1.0 - 0.5 * z + z * z * (
        4.166664568298827e-2 + z * (-1.388731625493765e-3 + z * 2.443315711809948e-5)
    )
    quadrant = turns.astype(jnp.int32)
    odd = (quadrant & 1) == 1
    sine = jnp.where(odd, c, s)
    cosine = jnp.where(odd, s, c)
    sine = jnp.where((quadrant & 2) == 2, -sine, sine)
    cosine = jnp.where(((quadrant + 1) & 2) == 2, -cosine, cosine)
    return sine, cosine


def exact_dot(x, y):
    return jnp.dot(x, y, precision=lax.Precision.HIGHEST, preferred_element_type=jnp.float32)


def slope_kernel(
    share, amplitude, valid, row_table, row_alt, col_table, gather, slopes, real, imag
):
    stars, rows, cols = share.shape
    subs = rows // PIX

    def per_sub(values):
        return jnp.sum(values.reshape(subs, PIX, cols), axis=1)

    power = amplitude[...]
    scale = exact_dot(per_sub(power * power), gather[...])
    scale = valid[...].astype(jnp.float32) / (scale * PAD)
    for g in range(stars):

        def step(i, carry):
            at = pl.ds(pl.multiple_of(i * PIX, PIX), PIX)
            sine, cosine = sine_cosine(share[g, at, :])
            amp = amplitude[at, :]
            real[at, :] = amp * cosine
            imag[at, :] = amp * sine
            return carry

        lax.fori_loop(0, subs, step, 0)
        a, b = real[...], imag[...]
        along = per_sub(a * exact_dot(row_table[...], b))
        alt_a, alt_b = exact_dot(row_alt[...], a)[:subs], exact_dot(row_alt[...], b)[:subs]
        down = 2.0 * along - PIX * (alt_a * alt_a + alt_b * alt_b)
        slopes[g, 0] = exact_dot(down, gather[...]) * scale
        pieces = []
        for k in range(cols // LANES):
            at = slice(k * LANES, (k + 1) * LANES)
            left, right = a[:, at], b[:, at]
            turned = exact_dot(right, col_table[...])
            other = exact_dot(left, col_table[:, LANES:])
            alt = turned[:, LANES:]
            pieces.append(2.0 * left * turned[:, :LANES] - (alt * alt + other * other))
        across = per_sub(jnp.concatenate(pieces, axis=1))
        slopes[g, 1] = exact_dot(across, gather[...]) * scale


def tables(rows, cols):
    def block_diagonal(count, block):
        return np.kron(np.eye(count), block)

    index = np.arange(PIX)
    gap = index[:, None] - index[None, :]
    angle = np.where(gap == 0, 1, gap) * (math.pi / PAD)
    sign = np.where(gap % 2 == 0, 1.0, -1.0)
    table = np.where(gap == 0, 0.0, PIX * sign * np.cos(angle) / np.sin(angle))
    alternate = np.where(index % 2 == 0, 1.0, -1.0)
    subs = rows // PIX
    row_table = block_diagonal(subs, table)
    row_alt = np.pad(block_diagonal(subs, alternate[None, :]), ((0, -subs % 8), (0, 0)))
    per = LANES // PIX
    spread = np.zeros((PIX, PIX))
    spread[:, 0] = 4.0 * alternate
    col_table = np.concatenate(
        [block_diagonal(per, table.T), block_diagonal(per, spread)], axis=1
    )
    gather = block_diagonal(cols // PIX, np.ones((PIX, 1)))
    return tuple(jnp.asarray(t, jnp.float32) for t in (row_table, row_alt, col_table, gather))


def slopes_of(share, amplitude, valid):
    stars, rows, cols = share.shape
    subs = valid.shape
    return pl.pallas_call(
        slope_kernel,
        out_shape=jax.ShapeDtypeStruct((stars, 2) + subs, jnp.float32),
        in_specs=[VMEM] * 7,
        out_specs=VMEM,
        scratch_shapes=[
            pltpu.VMEM((rows, cols), jnp.float32),
            pltpu.VMEM((rows, cols), jnp.float32),
        ],
        name="slopes",
    )(share, amplitude, valid, *tables(rows, cols))


def reduce_kernel(tiles, blocks, cores, terms, out, near, far, nsend, nrecv, fsend, frecv):
    tile, layer, core = (lax.axis_index(n) for n in ("tile", "layer", "star"))
    count = blocks * cores
    me = layer * cores + core
    near_peers = []
    for k in range(1, count):
        rank = lax.rem(me + k, count)
        near_peers.append({"layer": rank // cores, "star": lax.rem(rank, cores)})
    far_peers = [{"tile": lax.rem(tile + k, tiles)} for k in range(1, tiles)]
    greet(near_peers + far_peers)
    copies = []
    for k, peer in enumerate(near_peers):
        copy = pltpu.make_async_remote_copy(
            src_ref=terms,
            dst_ref=near.at[me],
            send_sem=nsend.at[k],
            recv_sem=nrecv.at[k],
            device_id=peer,
            device_id_type=MESH,
        )
        copy.start()
        copies.append(copy)
    near[me] = terms[...]
    for copy in copies:
        copy.wait()
    total = near[0]
    for k in range(1, count):
        total = total + near[k]
    far[tile] = total
    copies = []
    for k, peer in enumerate(far_peers):
        copy = pltpu.make_async_remote_copy(
            src_ref=far.at[tile],
            dst_ref=far.at[tile],
            send_sem=fsend.at[k],
            recv_sem=frecv.at[k],
            device_id=peer,
            device_id_type=MESH,
        )
        copy.start()
        copies.append(copy)
    for copy in copies:
        copy.wait()
    total = far[0]
    for k in range(1, tiles):
        total = total + far[k]
    out[...] = total


def reduce_all(terms):
    tiles, blocks, cores = (lax.axis_size(n) for n in ("tile", "layer", "star"))
    count = blocks * cores
    return pl.pallas_call(
        functools.partial(reduce_kernel, tiles, blocks, cores),
        out_shape=jax.ShapeDtypeStruct(terms.shape, jnp.float32),
        in_specs=[VMEM],
        out_specs=VMEM,
        scratch_shapes=[
            pltpu.VMEM((count,) + terms.shape, jnp.float32),
            pltpu.VMEM((tiles,) + terms.shape, jnp.float32),
            pltpu.SemaphoreType.DMA((count - 1,)),
            pltpu.SemaphoreType.DMA((count - 1,)),
            pltpu.SemaphoreType.DMA((tiles - 1,)),
            pltpu.SemaphoreType.DMA((tiles - 1,)),
        ],
        compiler_params=pltpu.CompilerParams(collective_id=2, has_side_effects=True),
        name="reduce",
    )(terms)


def body(
    screens,
    layer_weight,
    wind_row,
    wind_col,
    foot_row,
    foot_col,
    frac_row,
    frac_col,
    amplitude,
    valid,
    recon_matrix,
    prev_recon,
):
    lays = screens.shape[0]
    stars = recon_matrix.shape[0]
    layer_start = lax.axis_index("layer") * lays
    star_start = lax.axis_index("star") * stars

    def own(table):
        return lax.dynamic_slice(table, (star_start, layer_start), (stars, lays))

    def pairs(first, second):
        return jnp.stack([own(first), own(second)], axis=1).reshape(2 * stars, lays)

    winds = [lax.dynamic_slice_in_dim(w, layer_start, lays, 0)[None] for w in (wind_row, wind_col)]
    ints = jnp.concatenate(winds + [pairs(foot_row, foot_col)], axis=0)
    floats = jnp.concatenate([layer_weight[None], pairs(frac_row, frac_col)], axis=0)
    share, shifted = flow(ints, floats, screens, stars)
    slopes = slopes_of(share, amplitude, valid)
    local_terms = jnp.dot(
        slopes.astype(jnp.bfloat16).reshape(1, -1),
        recon_matrix.reshape(-1, recon_matrix.shape[-1]),
        preferred_element_type=jnp.float32,
    )
    recon = reduce_all(local_terms)[0]
    commands = 2.0 * recon - prev_recon
    return (shifted, slopes, commands)


def solution(mesh):
    return jax.shard_map(
        body,
        mesh=mesh,
        in_specs=(
            P(("runs", "layer"), "tile", None),
            P(("runs", "layer")),
            P("runs"),
            P("runs"),
            P(),
            P(),
            P(),
            P(),
            P("tile", "layer"),
            P("tile", "layer"),
            P("star", None, "tile", "layer", None),
            P("runs"),
        ),
        out_specs=(
            P(("runs", "layer"), "tile", None),
            P(("runs", "star"), None, "tile", "layer"),
            P("runs"),
        ),
        check_vma=False,
    )
```

```python
import functools
import math

import jax
import jax.numpy as jnp
import numpy as np
from jax import lax
from jax.experimental import pallas as pl
from jax.experimental.pallas import tpu as pltpu
from jax.sharding import PartitionSpec as P

PIX = 16
PAD = 32
WIND = 4
FOOT = 80
LANES = 128
HALO = -(-(WIND + FOOT + 1) // 8) * 8
MESH = pl.DeviceIdType.MESH
ANY = pl.BlockSpec(memory_space=pl.ANY)
SMEM = pl.BlockSpec(memory_space=pltpu.SMEM)
VMEM = pl.BlockSpec(memory_space=pltpu.VMEM)


def greet(peers):
    barrier = pltpu.get_barrier_semaphore()
    for peer in peers:
        pl.semaphore_signal(barrier, inc=1, device_id=peer, device_id_type=MESH)
    pl.semaphore_wait(barrier, len(peers))


def flow_kernel(
    tiles, cores, blocks, stars, weights, wind_row, wind_col, foot_row, foot_col,
    frac_row, frac_col, screens, share, shifted, field, land, outbox, inbox, zsend, zrecv, csend, crecv, xsend, xrecv, local,
):
    tile, core, layer = (lax.axis_index(n) for n in ("tile", "star", "layer"))
    up, down = lax.rem(tile + 1, tiles), lax.rem(tile + tiles - 1, tiles)
    partners = [lax.rem(core + k, cores) for k in range(1, cores)]
    peers = [lax.rem(layer + k, blocks) for k in range(1, blocks)]
    lays, rows, cols = screens.shape
    strips = cols // LANES
    per_block = strips // blocks
    unit = share.shape[2] // LANES // inbox.shape[1]
    units = inbox.shape[1]
    groups = rows // 8
    first = (layer + 1) * per_block + strips - 1
    star_start, layer_start = core * stars, layer * lays
    many = math.gcd(groups, 3)

    def column(n):
        return pl.ds(pl.multiple_of(lax.rem(first + n, strips) * LANES, LANES), LANES)

    copies = []
    for n in range(strips + 2):
        copy = pltpu.make_async_copy(
            screens.at[:, :, column(n % strips)],
            field.at[:, n, pl.ds(HALO, rows), :],
            local.at[n],
        )
        copy.start()
        copies.append(copy)
    greet(
        [{"tile": up}, {"tile": down}]
        + [{"star": p} for p in partners]
        + [{"layer": p} for p in peers]
    )
    sends = []
    for m in range(strips // cores):
        n = m * cores + core
        pair = []
        for d, (start, peer) in enumerate(((rows - HALO, up), (0, down))):
            copy = pltpu.make_async_remote_copy(
                src_ref=screens.at[:, pl.ds(start, HALO), column(n)],
                dst_ref=land.at[d, n],
                send_sem=zsend.at[m, d],
                recv_sem=zrecv.at[m, d],
                device_id={"tile": peer},
                device_id_type=MESH,
            )
            copy.start()
            pair.append(copy)
        sends.append(pair)
    for copy in copies:
        copy.wait()
    lane = lax.broadcasted_iota(jnp.int32, (8, LANES), 1)

    def window(j, row, base, n):
        return [field[j, base + n + k, pl.ds(row, 8), :] for k in range(unit + 1)]

    def place(start):
        base = start // LANES
        turn = start - base * LANES
        return base, turn

    def compute(u, store):
        low = u * unit

        def move_step(i, carry):
            for j in range(lays):
                base, turn = place(LANES - wind_col[layer_start + j])
                values = window(j, HALO + i * 8 - wind_row[layer_start + j], base, low)
                rolled = [pltpu.roll(v, (LANES - turn) & (LANES - 1), 1) for v in values]
                keep = lane < LANES - turn
                for k in range(unit):
                    shifted[j, pl.ds(pl.multiple_of(i * 8, 8), 8), column(low + k + 1)] = jnp.where(
                        keep, rolled[k], rolled[k + 1]
                    )
            return carry

        def pupil_step(n, carry):
            g = n // (groups // many)
            i = (n - g * (groups // many)) * many
            star = star_start + g
            total = [[None] * unit for _ in range(many)]
            for j in range(lays):
                lay = layer_start + j
                top_row = HALO + i * 8 + foot_row[star, lay] - wind_row[lay]
                base, turn = place(LANES + foot_col[star, lay] - wind_col[lay])
                weight = weights[j]
                a, b = frac_row[star, lay], frac_col[star, lay]
                top, bottom = weight * (1.0 - a), weight * a
                keep_near = lane < LANES - turn
                keep_far = lane < LANES - 1 - turn
                near_turn, far_turn = (LANES - turn) & (LANES - 1), LANES - 1 - turn
                for r in range(many):
                    row = top_row + r * 8
                    values = [
                        top * x + bottom * y
                        for x, y in zip(window(j, row, base, low), window(j, row + 1, base, low))
                    ]
                    near = [pltpu.roll(v, near_turn, 1) for v in values]
                    far = [pltpu.roll(v, far_turn, 1) for v in values]
                    for k in range(unit):
                        term = (1.0 - b) * jnp.where(
                            keep_near, near[k], near[k + 1]
                        ) + b * jnp.where(keep_far, far[k], far[k + 1])
                        total[r][k] = term if j == 0 else total[r][k] + term
            for r in range(many):
                for k in range(unit):
                    store(g, pl.ds(pl.multiple_of((i + r) * 8, 8), 8), k, total[r][k])
            return carry

        lax.fori_loop(0, stars * groups // many, pupil_step, 0)
        lax.fori_loop(0, groups, move_step, 0)

    def to_outbox(u):
        def store(g, at, k, value):
            outbox[u, g, at, k * LANES : (k + 1) * LANES] = value

        return store

    def to_share(u):
        def store(g, at, k, value):
            c = u * unit + k
            share[g, at, c * LANES : (c + 1) * LANES] = value

        return store

    forwards, swaps = [], []
    done = 0
    for m in range(strips // cores):
        n = m * cores + core
        current = []
        for d in range(2):
            sends[m][d].wait_recv()
            for k, p in enumerate(partners):
                forward = pltpu.make_async_remote_copy(
                    src_ref=land.at[d, n],
                    dst_ref=land.at[d, n],
                    send_sem=csend.at[m, d, k],
                    recv_sem=crecv.at[m, d, k],
                    device_id={"star": p},
                    device_id_type=MESH,
                )
                forward.start()
                current.append(forward)
        for forward in current:
            forward.wait_recv()
        forwards.extend(current)
        have = (m + 1) * cores
        for n in range(m * cores, have):
            for to in (n, n + strips):
                if to < strips + 2:
                    for j in range(lays):
                        field[j, to, 0:HALO, :] = land[0, n, j]
                        field[j, to, HALO + rows :, :] = land[1, n, j]
        while done < units * blocks and (
            have == strips or done * unit + unit + 2 <= have
        ):
            k, w = divmod(done, units)
            if k < blocks - 1:
                compute(done, to_outbox(done))
                copy = pltpu.make_async_remote_copy(
                    src_ref=outbox.at[done],
                    dst_ref=inbox.at[k, w],
                    send_sem=xsend.at[done],
                    recv_sem=xrecv.at[done],
                    device_id={"layer": peers[k]},
                    device_id_type=MESH,
                )
                copy.start()
                swaps.append(copy)
            else:
                compute(done, to_share(w))
            done += 1
    for n, copy in enumerate(swaps):
        k, w = divmod(n, units)
        copy.wait_recv()
        at = slice(w * unit * LANES, (w + 1) * unit * LANES)
        for g in range(stars):
            share[g, :, at] = share[g, :, at] + inbox[k, w, g]
    for pair in sends:
        for copy in pair:
            copy.wait_send()
    for copy in forwards + swaps:
        copy.wait_send()


def flow(scalars, screens, stars):
    tiles, blocks, cores = (lax.axis_size(n) for n in ("tile", "layer", "star"))
    lays, rows, cols = screens.shape
    strips = cols // LANES
    per_block = strips // blocks
    unit = 2 if per_block % 2 == 0 else 1
    units = per_block // unit
    width = cols // blocks
    steps = strips // cores
    dma = pltpu.SemaphoreType.DMA
    return pl.pallas_call(
        functools.partial(flow_kernel, tiles, cores, blocks, stars),
        out_shape=(
            jax.ShapeDtypeStruct((stars, rows, width), jnp.float32),
            jax.ShapeDtypeStruct((lays, rows, cols), jnp.float32),
        ),
        in_specs=[SMEM] * len(scalars) + [ANY],
        out_specs=(VMEM, VMEM),
        scratch_shapes=[
            pltpu.VMEM((lays, strips + 2, rows + 2 * HALO, LANES), jnp.float32),
            pltpu.VMEM((2, strips, lays, HALO, LANES), jnp.float32),
            pltpu.VMEM((units * (blocks - 1), stars, rows, unit * LANES), jnp.float32),
            pltpu.VMEM((blocks - 1, units, stars, rows, unit * LANES), jnp.float32),
            dma((steps, 2)),
            dma((steps, 2)),
            dma((steps, 2, cores - 1)),
            dma((steps, 2, cores - 1)),
            dma((units * (blocks - 1),)),
            dma((units * (blocks - 1),)),
            dma((strips + 2,)),
        ],
        compiler_params=pltpu.CompilerParams(collective_id=0, has_side_effects=True),
        name="flow",
    )(*scalars, screens)


def sine_cosine(x):
    turns = jnp.floor(x * (2.0 / math.pi) + 0.5)
    r = x - turns * 1.5703125
    r = r - turns * 4.837512969970703125e-4
    r = r - turns * 7.54978995489188216e-8
    z = r * r
    s = r + r * z * (-1.6666654611e-1 + z * (8.3321608736e-3 - z * 1.9515295891e-4))
    c = 1.0 - 0.5 * z + z * z * (
        4.166664568298827e-2 + z * (-1.388731625493765e-3 + z * 2.443315711809948e-5)
    )
    quadrant = turns.astype(jnp.int32)
    odd = (quadrant & 1) == 1
    sine = jnp.where(odd, c, s)
    cosine = jnp.where(odd, s, c)
    sine = jnp.where((quadrant & 2) == 2, -sine, sine)
    cosine = jnp.where(((quadrant + 1) & 2) == 2, -cosine, cosine)
    return sine, cosine


def halves(x):
    high = x.astype(jnp.bfloat16)
    return high, (x - high.astype(jnp.float32)).astype(jnp.bfloat16)


def product(x, y):
    return jnp.dot(x, y, preferred_element_type=jnp.float32)


def slope_kernel(
    share, amplitude, valid, row_high, row_low, row_alt, col_high, col_low, col_alt, gather,
    slopes, real, imag,
):
    stars, rows, cols = share.shape
    subs = rows // PIX

    def per_sub(values):
        return jnp.sum(values.reshape(subs, PIX, cols), axis=1)

    def collect(values):
        high, low = halves(values)
        return product(high, gather[...]) + product(low, gather[...])

    power = amplitude[...]
    scale = valid[...].astype(jnp.float32) / (collect(per_sub(power * power)) * PAD)
    for g in range(stars):

        def step(i, carry):
            at = pl.ds(pl.multiple_of(i * PIX, PIX), PIX)
            sine, cosine = sine_cosine(share[g, at, :])
            amp = amplitude[at, :]
            real[at, :] = amp * cosine
            imag[at, :] = amp * sine
            return carry

        lax.fori_loop(0, subs, step, 0)
        a, b = real[...], imag[...]
        a_high, a_low = halves(a)
        b_high, b_low = halves(b)
        turned = (
            product(row_high[...], b_high)
            + product(row_high[...], b_low)
            + product(row_low[...], b_high)
        )
        alt_a = (product(row_alt[...], a_high) + product(row_alt[...], a_low))[:subs]
        alt_b = (product(row_alt[...], b_high) + product(row_alt[...], b_low))[:subs]
        down = 2.0 * per_sub(a * turned) - PIX * (alt_a * alt_a + alt_b * alt_b)
        slopes[g, 0] = collect(down) * scale
        pieces = []
        for k in range(cols // LANES):
            at = slice(k * LANES, (k + 1) * LANES)
            turned = (
                product(b_high[:, at], col_high[...])
                + product(b_low[:, at], col_high[...])
                + product(b_high[:, at], col_low[...])
            )
            alt_a = product(a_high[:, at], col_alt[...]) + product(a_low[:, at], col_alt[...])
            alt_b = product(b_high[:, at], col_alt[...]) + product(b_low[:, at], col_alt[...])
            pieces.append(2.0 * a[:, at] * turned - (alt_a * alt_a + alt_b * alt_b))
        across = per_sub(jnp.concatenate(pieces, axis=1))
        slopes[g, 1] = collect(across) * scale


def tables(rows, cols):
    def block_diagonal(count, block):
        return np.kron(np.eye(count), block)

    index = np.arange(PIX)
    gap = index[:, None] - index[None, :]
    angle = np.where(gap == 0, 1, gap) * (math.pi / PAD)
    sign = np.where(gap % 2 == 0, 1.0, -1.0)
    table = np.where(gap == 0, 0.0, PIX * sign * np.cos(angle) / np.sin(angle))
    alternate = np.where(index % 2 == 0, 1.0, -1.0)
    subs = rows // PIX
    row_table = block_diagonal(subs, table)
    row_alt = np.pad(block_diagonal(subs, alternate[None, :]), ((0, -subs % 8), (0, 0)))
    per = LANES // PIX
    spread = np.zeros((PIX, PIX))
    spread[:, 0] = 4.0 * alternate
    col_table = block_diagonal(per, table.T)
    col_alt = block_diagonal(per, spread)
    gather = block_diagonal(cols // PIX, np.ones((PIX, 1)))

    def split(t):
        high = t.astype(jnp.bfloat16)
        return high, (t - high.astype(np.float64)).astype(jnp.bfloat16)

    exact = [t.astype(jnp.bfloat16) for t in (row_alt, col_alt, gather)]
    parts = (*split(row_table), exact[0], *split(col_table), exact[1], exact[2])
    return tuple(jnp.asarray(t) for t in parts)


def slopes_of(share, amplitude, valid):
    stars, rows, cols = share.shape
    subs = valid.shape
    return pl.pallas_call(
        slope_kernel,
        out_shape=jax.ShapeDtypeStruct((stars, 2) + subs, jnp.float32),
        in_specs=[VMEM] * 10,
        out_specs=VMEM,
        scratch_shapes=[
            pltpu.VMEM((rows, cols), jnp.float32),
            pltpu.VMEM((rows, cols), jnp.float32),
        ],
        name="slopes",
    )(share, amplitude, valid, *tables(rows, cols))


def reduce_kernel(tiles, blocks, cores, terms, out, near, far, nsend, nrecv, fsend, frecv):
    tile, layer, core = (lax.axis_index(n) for n in ("tile", "layer", "star"))
    count = blocks * cores
    me = layer * cores + core
    near_peers = []
    for k in range(1, count):
        rank = lax.rem(me + k, count)
        near_peers.append({"layer": rank // cores, "star": lax.rem(rank, cores)})
    far_peers = [{"tile": lax.rem(tile + k, tiles)} for k in range(1, tiles)]
    greet(near_peers + far_peers)
    copies = []
    for k, peer in enumerate(near_peers):
        copy = pltpu.make_async_remote_copy(
            src_ref=terms,
            dst_ref=near.at[me],
            send_sem=nsend.at[k],
            recv_sem=nrecv.at[k],
            device_id=peer,
            device_id_type=MESH,
        )
        copy.start()
        copies.append(copy)
    near[me] = terms[...]
    for copy in copies:
        copy.wait()
    total = near[0]
    for k in range(1, count):
        total = total + near[k]
    far[tile] = total
    copies = []
    for k, peer in enumerate(far_peers):
        copy = pltpu.make_async_remote_copy(
            src_ref=far.at[tile],
            dst_ref=far.at[tile],
            send_sem=fsend.at[k],
            recv_sem=frecv.at[k],
            device_id=peer,
            device_id_type=MESH,
        )
        copy.start()
        copies.append(copy)
    for copy in copies:
        copy.wait()
    total = far[0]
    for k in range(1, tiles):
        total = total + far[k]
    out[...] = total


def reduce_all(terms):
    tiles, blocks, cores = (lax.axis_size(n) for n in ("tile", "layer", "star"))
    count = blocks * cores
    return pl.pallas_call(
        functools.partial(reduce_kernel, tiles, blocks, cores),
        out_shape=jax.ShapeDtypeStruct(terms.shape, jnp.float32),
        in_specs=[VMEM],
        out_specs=VMEM,
        scratch_shapes=[
            pltpu.VMEM((count,) + terms.shape, jnp.float32),
            pltpu.VMEM((tiles,) + terms.shape, jnp.float32),
            pltpu.SemaphoreType.DMA((count - 1,)),
            pltpu.SemaphoreType.DMA((count - 1,)),
            pltpu.SemaphoreType.DMA((tiles - 1,)),
            pltpu.SemaphoreType.DMA((tiles - 1,)),
        ],
        compiler_params=pltpu.CompilerParams(collective_id=2, has_side_effects=True),
        name="reduce",
    )(terms)


def body(
    screens,
    layer_weight,
    wind_row,
    wind_col,
    foot_row,
    foot_col,
    frac_row,
    frac_col,
    amplitude,
    valid,
    recon_matrix,
    prev_recon,
):
    stars = recon_matrix.shape[0]
    scalars = (layer_weight, wind_row, wind_col, foot_row, foot_col, frac_row, frac_col)
    share, shifted = flow(scalars, screens, stars)
    slopes = slopes_of(share, amplitude, valid)
    local_terms = jnp.dot(
        slopes.astype(jnp.bfloat16).reshape(1, -1),
        recon_matrix.reshape(-1, recon_matrix.shape[-1]),
        preferred_element_type=jnp.float32,
    )
    recon = reduce_all(local_terms)[0]
    commands = 2.0 * recon - prev_recon
    return (shifted, slopes, commands)


def solution(mesh):
    return jax.shard_map(
        body,
        mesh=mesh,
        in_specs=(
            P(("runs", "layer"), "tile", None),
            P(("runs", "layer")),
            P("runs"),
            P("runs"),
            P(),
            P(),
            P(),
            P(),
            P("tile", "layer"),
            P("tile", "layer"),
            P("star", None, "tile", "layer", None),
            P("runs"),
        ),
        out_specs=(
            P(("runs", "layer"), "tile", None),
            P(("runs", "star"), None, "tile", "layer"),
            P("runs"),
        ),
        check_vma=False,
    )
```

```python
import functools
import math

import jax
import jax.numpy as jnp
import numpy as np
from jax import lax
from jax.experimental import pallas as pl
from jax.experimental.pallas import tpu as pltpu
from jax.sharding import PartitionSpec as P

PIX = 16
PAD = 32
WIND = 4
FOOT = 80
LANES = 128
HALO = -(-(WIND + FOOT + 1) // 8) * 8
MESH = pl.DeviceIdType.MESH
ANY = pl.BlockSpec(memory_space=pl.ANY)
SMEM = pl.BlockSpec(memory_space=pltpu.SMEM)
VMEM = pl.BlockSpec(memory_space=pltpu.VMEM)


def greet(peers):
    barrier = pltpu.get_barrier_semaphore()
    for peer in peers:
        pl.semaphore_signal(barrier, inc=1, device_id=peer, device_id_type=MESH)
    pl.semaphore_wait(barrier, len(peers))


def flow_kernel(
    tiles, cores, blocks, stars, weights, wind_row, wind_col, foot_row, foot_col,
    frac_row, frac_col, screens, share, shifted, field, land, outbox, inbox, zsend, zrecv, csend, crecv, xsend, xrecv, local,
):
    tile, core, layer = (lax.axis_index(n) for n in ("tile", "star", "layer"))
    up, down = lax.rem(tile + 1, tiles), lax.rem(tile + tiles - 1, tiles)
    partners = [lax.rem(core + k, cores) for k in range(1, cores)]
    peers = [lax.rem(layer + k, blocks) for k in range(1, blocks)]
    lays, rows, cols = screens.shape
    strips = cols // LANES
    per_block = strips // blocks
    unit = share.shape[2] // LANES // inbox.shape[1]
    units = inbox.shape[1]
    groups = rows // 8
    first = (layer + 1) * per_block + strips - 1
    star_start, layer_start = core * stars, layer * lays
    many = math.gcd(groups, 6)

    def column(n):
        return pl.ds(pl.multiple_of(lax.rem(first + n, strips) * LANES, LANES), LANES)

    copies = []
    for n in range(strips + 2):
        copy = pltpu.make_async_copy(
            screens.at[:, :, column(n % strips)],
            field.at[:, n, pl.ds(HALO, rows), :],
            local.at[n],
        )
        copy.start()
        copies.append(copy)
    greet(
        [{"tile": up}, {"tile": down}]
        + [{"star": p} for p in partners]
        + [{"layer": p} for p in peers]
    )
    sends = []
    for m in range(strips // cores):
        n = m * cores + core
        pair = []
        for d, (start, peer) in enumerate(((rows - HALO, up), (0, down))):
            copy = pltpu.make_async_remote_copy(
                src_ref=screens.at[:, pl.ds(start, HALO), column(n)],
                dst_ref=land.at[d, n],
                send_sem=zsend.at[m, d],
                recv_sem=zrecv.at[m, d],
                device_id={"tile": peer},
                device_id_type=MESH,
            )
            copy.start()
            pair.append(copy)
        sends.append(pair)
    for copy in copies:
        copy.wait()
    lane = lax.broadcasted_iota(jnp.int32, (8, LANES), 1)

    def window(j, row, base, n):
        return [field[j, base + n + k, pl.ds(row, 8), :] for k in range(unit + 1)]

    def place(start):
        base = start // LANES
        turn = start - base * LANES
        return base, turn

    def compute(u, store):
        low = u * unit

        def move_step(i, carry):
            for j in range(lays):
                base, turn = place(LANES - wind_col[layer_start + j])
                values = window(j, HALO + i * 8 - wind_row[layer_start + j], base, low)
                rolled = [pltpu.roll(v, (LANES - turn) & (LANES - 1), 1) for v in values]
                keep = lane < LANES - turn
                for k in range(unit):
                    shifted[j, pl.ds(pl.multiple_of(i * 8, 8), 8), column(low + k + 1)] = jnp.where(
                        keep, rolled[k], rolled[k + 1]
                    )
            return carry

        def pupil_step(n, carry):
            g = n // (groups // many)
            i = (n - g * (groups // many)) * many
            star = star_start + g
            total = [[None] * unit for _ in range(many)]
            for j in range(lays):
                lay = layer_start + j
                top_row = HALO + i * 8 + foot_row[star, lay] - wind_row[lay]
                base, turn = place(LANES + foot_col[star, lay] - wind_col[lay])
                weight = weights[j]
                a, b = frac_row[star, lay], frac_col[star, lay]
                top, bottom = weight * (1.0 - a), weight * a
                keep_near = lane < LANES - turn
                keep_far = lane < LANES - 1 - turn
                near_turn, far_turn = (LANES - turn) & (LANES - 1), LANES - 1 - turn
                for r in range(many):
                    row = top_row + r * 8
                    values = [
                        top * x + bottom * y
                        for x, y in zip(window(j, row, base, low), window(j, row + 1, base, low))
                    ]
                    near = [pltpu.roll(v, near_turn, 1) for v in values]
                    far = [pltpu.roll(v, far_turn, 1) for v in values]
                    for k in range(unit):
                        term = (1.0 - b) * jnp.where(
                            keep_near, near[k], near[k + 1]
                        ) + b * jnp.where(keep_far, far[k], far[k + 1])
                        total[r][k] = term if j == 0 else total[r][k] + term
            for r in range(many):
                for k in range(unit):
                    store(g, pl.ds(pl.multiple_of((i + r) * 8, 8), 8), k, total[r][k])
            return carry

        lax.fori_loop(0, stars * groups // many, pupil_step, 0)
        lax.fori_loop(0, groups, move_step, 0, unroll=math.gcd(groups, 3))

    def to_outbox(u):
        def store(g, at, k, value):
            outbox[u, g, at, k * LANES : (k + 1) * LANES] = value

        return store

    def to_share(u):
        def store(g, at, k, value):
            c = u * unit + k
            share[g, at, c * LANES : (c + 1) * LANES] = value

        return store

    forwards, swaps = [], []
    done = 0
    for m in range(strips // cores):
        n = m * cores + core
        current = []
        for d in range(2):
            sends[m][d].wait_recv()
            for k, p in enumerate(partners):
                forward = pltpu.make_async_remote_copy(
                    src_ref=land.at[d, n],
                    dst_ref=land.at[d, n],
                    send_sem=csend.at[m, d, k],
                    recv_sem=crecv.at[m, d, k],
                    device_id={"star": p},
                    device_id_type=MESH,
                )
                forward.start()
                current.append(forward)
        for forward in current:
            forward.wait_recv()
        forwards.extend(current)
        have = (m + 1) * cores
        for n in range(m * cores, have):
            for to in (n, n + strips):
                if to < strips + 2:
                    for j in range(lays):
                        field[j, to, 0:HALO, :] = land[0, n, j]
                        field[j, to, HALO + rows :, :] = land[1, n, j]
        while done < units * blocks and (
            have == strips or done * unit + unit + 2 <= have
        ):
            k, w = divmod(done, units)
            if k < blocks - 1:
                compute(done, to_outbox(done))
                copy = pltpu.make_async_remote_copy(
                    src_ref=outbox.at[done],
                    dst_ref=inbox.at[k, w],
                    send_sem=xsend.at[done],
                    recv_sem=xrecv.at[done],
                    device_id={"layer": peers[k]},
                    device_id_type=MESH,
                )
                copy.start()
                swaps.append(copy)
            else:
                compute(done, to_share(w))
            done += 1
    for n, copy in enumerate(swaps):
        k, w = divmod(n, units)
        copy.wait_recv()
        at = slice(w * unit * LANES, (w + 1) * unit * LANES)
        for g in range(stars):
            share[g, :, at] = share[g, :, at] + inbox[k, w, g]
    for pair in sends:
        for copy in pair:
            copy.wait_send()
    for copy in forwards + swaps:
        copy.wait_send()


def flow(scalars, screens, stars):
    tiles, blocks, cores = (lax.axis_size(n) for n in ("tile", "layer", "star"))
    lays, rows, cols = screens.shape
    strips = cols // LANES
    per_block = strips // blocks
    unit = 2 if per_block % 2 == 0 else 1
    units = per_block // unit
    width = cols // blocks
    steps = strips // cores
    dma = pltpu.SemaphoreType.DMA
    return pl.pallas_call(
        functools.partial(flow_kernel, tiles, cores, blocks, stars),
        out_shape=(
            jax.ShapeDtypeStruct((stars, rows, width), jnp.float32),
            jax.ShapeDtypeStruct((lays, rows, cols), jnp.float32),
        ),
        in_specs=[SMEM] * len(scalars) + [ANY],
        out_specs=(VMEM, VMEM),
        scratch_shapes=[
            pltpu.VMEM((lays, strips + 2, rows + 2 * HALO, LANES), jnp.float32),
            pltpu.VMEM((2, strips, lays, HALO, LANES), jnp.float32),
            pltpu.VMEM((units * (blocks - 1), stars, rows, unit * LANES), jnp.float32),
            pltpu.VMEM((blocks - 1, units, stars, rows, unit * LANES), jnp.float32),
            dma((steps, 2)),
            dma((steps, 2)),
            dma((steps, 2, cores - 1)),
            dma((steps, 2, cores - 1)),
            dma((units * (blocks - 1),)),
            dma((units * (blocks - 1),)),
            dma((strips + 2,)),
        ],
        compiler_params=pltpu.CompilerParams(collective_id=0, has_side_effects=True),
        name="flow",
    )(*scalars, screens)


def sine_cosine(x):
    turns = jnp.floor(x * (2.0 / math.pi) + 0.5)
    r = x - turns * 1.5703125
    r = r - turns * 4.837512969970703125e-4
    r = r - turns * 7.54978995489188216e-8
    z = r * r
    s = r + r * z * (-1.6666654611e-1 + z * (8.3321608736e-3 - z * 1.9515295891e-4))
    c = 1.0 - 0.5 * z + z * z * (
        4.166664568298827e-2 + z * (-1.388731625493765e-3 + z * 2.443315711809948e-5)
    )
    quadrant = turns.astype(jnp.int32)
    odd = (quadrant & 1) == 1
    sine = jnp.where(odd, c, s)
    cosine = jnp.where(odd, s, c)
    sine = jnp.where((quadrant & 2) == 2, -sine, sine)
    cosine = jnp.where(((quadrant + 1) & 2) == 2, -cosine, cosine)
    return sine, cosine


def halves(x):
    high = x.astype(jnp.bfloat16)
    return high, (x - high.astype(jnp.float32)).astype(jnp.bfloat16)


def product(x, y):
    return jnp.dot(x, y, preferred_element_type=jnp.float32)


def slope_kernel(
    share, amplitude, valid, row_high, row_low, row_alt, col_high, col_low, col_alt, gather,
    slopes, real, imag,
):
    stars, rows, cols = share.shape
    subs = rows // PIX

    def per_sub(values):
        return jnp.sum(values.reshape(subs, PIX, cols), axis=1)

    def collect(values):
        high, low = halves(values)
        return product(high, gather[...]) + product(low, gather[...])

    power = amplitude[...]
    scale = valid[...].astype(jnp.float32) / (collect(per_sub(power * power)) * PAD)
    for g in range(stars):

        def step(i, carry):
            at = pl.ds(pl.multiple_of(i * PIX, PIX), PIX)
            sine, cosine = sine_cosine(share[g, at, :])
            amp = amplitude[at, :]
            real[at, :] = amp * cosine
            imag[at, :] = amp * sine
            return carry

        lax.fori_loop(0, subs, step, 0)
        a, b = real[...], imag[...]
        a_high, a_low = halves(a)
        b_high, b_low = halves(b)
        turned = (
            product(row_high[...], b_high)
            + product(row_high[...], b_low)
            + product(row_low[...], b_high)
        )
        alt_a = (product(row_alt[...], a_high) + product(row_alt[...], a_low))[:subs]
        alt_b = (product(row_alt[...], b_high) + product(row_alt[...], b_low))[:subs]
        down = 2.0 * per_sub(a * turned) - PIX * (alt_a * alt_a + alt_b * alt_b)
        slopes[g, 0] = collect(down) * scale
        pieces = []
        for k in range(cols // LANES):
            at = slice(k * LANES, (k + 1) * LANES)
            turned = (
                product(b_high[:, at], col_high[...])
                + product(b_low[:, at], col_high[...])
                + product(b_high[:, at], col_low[...])
            )
            alt_a = product(a_high[:, at], col_alt[...]) + product(a_low[:, at], col_alt[...])
            alt_b = product(b_high[:, at], col_alt[...]) + product(b_low[:, at], col_alt[...])
            pieces.append(2.0 * a[:, at] * turned - (alt_a * alt_a + alt_b * alt_b))
        across = per_sub(jnp.concatenate(pieces, axis=1))
        slopes[g, 1] = collect(across) * scale


def tables(rows, cols):
    def block_diagonal(count, block):
        return np.kron(np.eye(count), block)

    index = np.arange(PIX)
    gap = index[:, None] - index[None, :]
    angle = np.where(gap == 0, 1, gap) * (math.pi / PAD)
    sign = np.where(gap % 2 == 0, 1.0, -1.0)
    table = np.where(gap == 0, 0.0, PIX * sign * np.cos(angle) / np.sin(angle))
    alternate = np.where(index % 2 == 0, 1.0, -1.0)
    subs = rows // PIX
    row_table = block_diagonal(subs, table)
    row_alt = np.pad(block_diagonal(subs, alternate[None, :]), ((0, -subs % 8), (0, 0)))
    per = LANES // PIX
    spread = np.zeros((PIX, PIX))
    spread[:, 0] = 4.0 * alternate
    col_table = block_diagonal(per, table.T)
    col_alt = block_diagonal(per, spread)
    gather = block_diagonal(cols // PIX, np.ones((PIX, 1)))

    def split(t):
        high = t.astype(jnp.bfloat16)
        return high, (t - high.astype(np.float64)).astype(jnp.bfloat16)

    exact = [t.astype(jnp.bfloat16) for t in (row_alt, col_alt, gather)]
    parts = (*split(row_table), exact[0], *split(col_table), exact[1], exact[2])
    return tuple(jnp.asarray(t) for t in parts)


def slopes_of(share, amplitude, valid):
    stars, rows, cols = share.shape
    subs = valid.shape
    return pl.pallas_call(
        slope_kernel,
        out_shape=jax.ShapeDtypeStruct((stars, 2) + subs, jnp.float32),
        in_specs=[VMEM] * 10,
        out_specs=VMEM,
        scratch_shapes=[
            pltpu.VMEM((rows, cols), jnp.float32),
            pltpu.VMEM((rows, cols), jnp.float32),
        ],
        name="slopes",
    )(share, amplitude, valid, *tables(rows, cols))


def reduce_kernel(tiles, blocks, cores, terms, out, near, far, nsend, nrecv, fsend, frecv):
    tile, layer, core = (lax.axis_index(n) for n in ("tile", "layer", "star"))
    count = blocks * cores
    me = layer * cores + core
    near_peers = []
    for k in range(1, count):
        rank = lax.rem(me + k, count)
        near_peers.append({"layer": rank // cores, "star": lax.rem(rank, cores)})
    far_peers = [{"tile": lax.rem(tile + k, tiles)} for k in range(1, tiles)]
    greet(near_peers + far_peers)
    copies = []
    for k, peer in enumerate(near_peers):
        copy = pltpu.make_async_remote_copy(
            src_ref=terms,
            dst_ref=near.at[me],
            send_sem=nsend.at[k],
            recv_sem=nrecv.at[k],
            device_id=peer,
            device_id_type=MESH,
        )
        copy.start()
        copies.append(copy)
    near[me] = terms[...]
    for copy in copies:
        copy.wait()
    total = near[0]
    for k in range(1, count):
        total = total + near[k]
    far[tile] = total
    copies = []
    for k, peer in enumerate(far_peers):
        copy = pltpu.make_async_remote_copy(
            src_ref=far.at[tile],
            dst_ref=far.at[tile],
            send_sem=fsend.at[k],
            recv_sem=frecv.at[k],
            device_id=peer,
            device_id_type=MESH,
        )
        copy.start()
        copies.append(copy)
    for copy in copies:
        copy.wait()
    total = far[0]
    for k in range(1, tiles):
        total = total + far[k]
    out[...] = total


def reduce_all(terms):
    tiles, blocks, cores = (lax.axis_size(n) for n in ("tile", "layer", "star"))
    count = blocks * cores
    return pl.pallas_call(
        functools.partial(reduce_kernel, tiles, blocks, cores),
        out_shape=jax.ShapeDtypeStruct(terms.shape, jnp.float32),
        in_specs=[VMEM],
        out_specs=VMEM,
        scratch_shapes=[
            pltpu.VMEM((count,) + terms.shape, jnp.float32),
            pltpu.VMEM((tiles,) + terms.shape, jnp.float32),
            pltpu.SemaphoreType.DMA((count - 1,)),
            pltpu.SemaphoreType.DMA((count - 1,)),
            pltpu.SemaphoreType.DMA((tiles - 1,)),
            pltpu.SemaphoreType.DMA((tiles - 1,)),
        ],
        compiler_params=pltpu.CompilerParams(collective_id=2, has_side_effects=True),
        name="reduce",
    )(terms)


def body(
    screens,
    layer_weight,
    wind_row,
    wind_col,
    foot_row,
    foot_col,
    frac_row,
    frac_col,
    amplitude,
    valid,
    recon_matrix,
    prev_recon,
):
    stars = recon_matrix.shape[0]
    scalars = (layer_weight, wind_row, wind_col, foot_row, foot_col, frac_row, frac_col)
    share, shifted = flow(scalars, screens, stars)
    slopes = slopes_of(share, amplitude, valid)
    local_terms = jnp.dot(
        slopes.astype(jnp.bfloat16).reshape(1, -1),
        recon_matrix.reshape(-1, recon_matrix.shape[-1]),
        preferred_element_type=jnp.float32,
    )
    recon = reduce_all(local_terms)[0]
    commands = 2.0 * recon - prev_recon
    return (shifted, slopes, commands)


def solution(mesh):
    return jax.shard_map(
        body,
        mesh=mesh,
        in_specs=(
            P(("runs", "layer"), "tile", None),
            P(("runs", "layer")),
            P("runs"),
            P("runs"),
            P(),
            P(),
            P(),
            P(),
            P("tile", "layer"),
            P("tile", "layer"),
            P("star", None, "tile", "layer", None),
            P("runs"),
        ),
        out_specs=(
            P(("runs", "layer"), "tile", None),
            P(("runs", "star"), None, "tile", "layer"),
            P("runs"),
        ),
        check_vma=False,
    )
```
